32 devices in a mesh: section: 4 (over z), seq: 4 (over y, x), tp: 2 (over core).
Axes of the slice: x: 2, y: 2, z: 4, core: 2. Of those that a mesh axis runs over, the one named last changes fastest.
Arguments:
- queries: bfloat16 [4, 512, 8192], P('section', 'seq', 'tp'), may hold values from -64 to 64
- picture_key_matrix: bfloat16 [4, 32, 1024], P('section', ('seq', 'tp')), may hold values from -8 to 8
- picture_value_matrix: bfloat16 [4, 32, 1024], P('section', ('seq', 'tp')), may hold values from -6 to 6
- cotangent: bfloat16 [4, 512, 8192], P('section', 'seq', 'tp'), may hold values from -6 to 6
- pattern: int32 [4, 4, 4], P('section', 'seq'), may hold values from 0 to 1, as said below
- tile_owner: int32 [4, 4], P('section'), may hold values from 0 to 3, each once within a row
Outputs:
- attended: bfloat16 [4, 512, 8192], P('section', 'seq', 'tp')
- grad_queries: bfloat16 [4, 512, 8192], P('section', 'seq', 'tp')
- grad_keys: bfloat16 [4, 32, 1024], P('section', 'seq', 'tp')
- grad_values: bfloat16 [4, 32, 1024], P('section', 'seq', 'tp')
The draws below stay inside these ranges and needn't reach their ends.
Inputs may be any that keep to these rules, and one draw needn't show every extreme that they name: `pattern`: every text block attends to at least one and at most four tiles. `tile_owner`: each slot's row is a permutation: every row block holds exactly one tile.
All inputs are finite; a program needn't handle non-finite values.
Results may differ from the reference program's by a relative error of at most 0.0092.
Values may be sent and summed in bfloat16 or wider, within the bound.
A program may use at most 64 MiB of HBM per device.

```python
import jax
import jax.numpy as jnp
from jax import lax

QUERY_HEADS = 64
KEY_VALUE_HEADS = 8
HEAD_SIZE = 128
TILE_TOK = 8
BLOCK = 128
TEXT = 512
TILES = 4
IMAGE_TOKENS = 32
TEXT_BLOCKS = 4
N_SECTION = 4


def draw_pair(key):
    base = jax.random.fold_in(key, 31)
    key_query, random_key_split = jax.random.split(base, 2)
    picture_key_matrix = jax.random.normal(random_key_split, (N_SECTION, IMAGE_TOKENS, KEY_VALUE_HEADS * HEAD_SIZE), jnp.float32)
    queries = jax.random.normal(key_query, (N_SECTION, TEXT, QUERY_HEADS * HEAD_SIZE), jnp.float32)
    return (queries, picture_key_matrix)


def draw_queries(key, part):
    return draw_pair(key)[0].astype(jnp.bfloat16)


def draw_picture_key_matrix(key, part):
    return draw_pair(key)[1].astype(jnp.bfloat16)


def draw_pattern(key, part):
    base = jax.random.fold_in(key, 5)
    key_count, key_score = jax.random.split(base, 2)
    most = min(4, TILES)
    counts = jax.random.randint(key_count, (N_SECTION, TEXT_BLOCKS, 1), 1, most + 1)
    scores = jax.random.randint(key_score, (N_SECTION, TEXT_BLOCKS, TILES), 0, 1 << 20) * TILES + jnp.arange(TILES, dtype=jnp.int32)[None, None, :]
    ranks = jnp.argsort(jnp.argsort(scores, axis=-1), axis=-1)
    return (ranks < counts).astype(jnp.int32)


def block_levels(stream_key, dims, pieces, least, top_value):
    def one(position, shards_of):
        draws = jax.random.uniform(jax.random.fold_in(jax.random.fold_in(stream_key, 6), position), (shards_of,), jnp.float32, least / len(pieces), top_value / len(pieces))
        return jnp.repeat(jnp.exp(draws), dims[position] // shards_of).reshape((-1,) + (1,) * (len(dims) - position - 1))

    level = one(*pieces[0])
    for cut in pieces[1:]:
        level = level * one(*cut)
    return level


def gaussian(stream_key, extent, spread, most, shards=(), kind=jnp.bfloat16):
    drawn = jax.random.normal(stream_key, extent, jnp.float32) * spread
    if len(shards) > 0:
        drawn = block_levels(stream_key, extent, shards, -0.22, 0.18) * drawn
    return jnp.clip(drawn, min=-most, max=most).astype(kind)


def setup_inputs(seed: int = 0) -> dict:
    seeds = jax.random.split(jax.random.key(seed), 7)
    return {
        "queries": draw_queries(jax.random.fold_in(seeds[6], 71), 0),
        "picture_key_matrix": draw_picture_key_matrix(jax.random.fold_in(seeds[6], 71), 0),
        "picture_value_matrix": gaussian(seeds[2], (N_SECTION, IMAGE_TOKENS, KEY_VALUE_HEADS * HEAD_SIZE), 1.0, 6.0, ((0, 4), (1, 8))),
        "cotangent": gaussian(seeds[3], (N_SECTION, TEXT, QUERY_HEADS * HEAD_SIZE), 1.0, 6.0, ((0, 4), (1, 4), (2, 2))),
        "pattern": draw_pattern(jax.random.fold_in(seeds[6], 71), 0),
        "tile_owner": jax.vmap(lambda own: jax.random.permutation(own, TILES))(jax.random.split(seeds[5], N_SECTION)).reshape((N_SECTION, TILES)).astype(jnp.int32),
    }


def token_mask(pattern_slot, owner_slot):
    hits = (owner_slot[:, None] == jnp.arange(TILES, dtype=jnp.int32)[None, :]).astype(jnp.float32)
    allowed = jnp.dot(pattern_slot.astype(jnp.float32), hits) > 0.5
    return jnp.repeat(jnp.repeat(allowed, BLOCK, axis=0), TILE_TOK, axis=1)


def attend_group(query_group, key_group, value_group, cot_group, mask):
    scale = HEAD_SIZE ** -0.5
    scores = jnp.einsum('thd,jd->htj', query_group, key_group) * scale
    scores = jnp.where(mask[None], scores, -jnp.inf)
    top = jnp.max(scores, axis=-1, keepdims=True)
    expo = jnp.exp(scores - top)
    probs = expo / jnp.sum(expo, axis=-1, keepdims=True)
    probs_low = lax.optimization_barrier(probs.astype(jnp.bfloat16)).astype(jnp.float32)
    output = jnp.einsum('htj,jd->thd', probs_low, value_group)
    out_low = lax.optimization_barrier(output.astype(jnp.bfloat16))
    delta = jnp.einsum('thd,thd->ht', cot_group, out_low.astype(jnp.float32))
    dprobs = jnp.einsum('thd,jd->htj', cot_group, value_group)
    dscores = probs * (dprobs - delta[:, :, None])
    ds_low = lax.optimization_barrier(dscores.astype(jnp.bfloat16)).astype(jnp.float32)
    grad_query = (jnp.einsum('htj,jd->thd', ds_low, key_group) * scale).astype(jnp.bfloat16)
    grad_key = jnp.einsum('htj,thd->jd', ds_low, query_group) * scale
    grad_value = jnp.einsum('htj,thd->jd', probs_low, cot_group)
    return out_low, grad_query, grad_key, grad_value


def one_slot(items):
    queries, picture_key_matrix, picture_value_matrix, rolled, pattern, tile_owner = items
    mask = token_mask(pattern, tile_owner)
    head_group = QUERY_HEADS // KEY_VALUE_HEADS
    outs, grad_qs, grad_ks, grad_vs = [], [], [], []
    for key_value_head in range(KEY_VALUE_HEADS):
        query_group = queries[:, key_value_head * head_group * HEAD_SIZE:(key_value_head + 1) * head_group * HEAD_SIZE].astype(jnp.float32).reshape(TEXT, head_group, HEAD_SIZE)
        cot_group = rolled[:, key_value_head * head_group * HEAD_SIZE:(key_value_head + 1) * head_group * HEAD_SIZE].astype(jnp.float32).reshape(TEXT, head_group, HEAD_SIZE)
        key_group = picture_key_matrix[:, key_value_head * HEAD_SIZE:(key_value_head + 1) * HEAD_SIZE].astype(jnp.float32)
        value_group = picture_value_matrix[:, key_value_head * HEAD_SIZE:(key_value_head + 1) * HEAD_SIZE].astype(jnp.float32)
        out_low, grad_query, grad_key, grad_value = attend_group(query_group, key_group, value_group, cot_group, mask)
        outs.append(out_low.reshape(TEXT, head_group * HEAD_SIZE))
        grad_qs.append(grad_query.reshape(TEXT, head_group * HEAD_SIZE))
        grad_ks.append(grad_key)
        grad_vs.append(grad_value)
    return (jnp.concatenate(outs, 1), jnp.concatenate(grad_qs, 1),
            jnp.concatenate(grad_ks, 1).astype(jnp.bfloat16), jnp.concatenate(grad_vs, 1).astype(jnp.bfloat16))


def reference(queries, picture_key_matrix, picture_value_matrix, cotangent, pattern, tile_owner):
    rolled = jnp.roll(cotangent, -1, axis=0)
    attended, grad_queries, grad_keys, grad_values = lax.map(one_slot, (queries, picture_key_matrix, picture_value_matrix, rolled, pattern, tile_owner))
    return attended, grad_queries, grad_keys, grad_values
```

```python
import functools

import jax
import jax.numpy as jnp
from jax import lax
from jax.experimental import pallas as pl
from jax.experimental.pallas import tpu as pltpu
from jax.sharding import PartitionSpec as P

QUERY_HEADS = 64
KEY_VALUE_HEADS = 8
HEAD_SIZE = 128
FAN = QUERY_HEADS // KEY_VALUE_HEADS
PACK = 4
CUTS = 4
MESH = pl.DeviceIdType.MESH
F32 = jnp.float32
BF16 = jnp.bfloat16


def nt(a, b):
    return lax.dot_general(a, b, (((1,), (1,)), ((), ())), preferred_element_type=F32)


def nn(a, b):
    return lax.dot_general(a, b, (((1,), (0,)), ((), ())), preferred_element_type=F32)


def tn(a, b):
    return lax.dot_general(a, b, (((0,), (0,)), ((), ())), preferred_element_type=F32)


def kernel(
    nsec, nseq, ntp,
    q_hbm, k_hbm, v_hbm, c_hbm, pat, own,
    att_vm, gq_vm, gk_out, gv_out,
    q_vm, c_vm,
    kg, vg, ng, asm, k_bd, v_bd,
    p_f32, p_send, p_recv, dp_send, dp_recv,
    dk_t, dv_t, dk_r, dv_r,
    load_sem, own_sem,
    k_ss, k_rs, v_ss, v_rs, n_ss, n_rs,
    p_ss, p_rs, dp_ss, dp_rs,
    dk_ss, dk_rs, dv_ss, dv_rs,
):
    scale = HEAD_SIZE ** (-0.5)
    D = HEAD_SIZE
    n = nseq * ntp
    text, cols = q_vm.shape
    part = k_hbm.shape[1]
    width = k_hbm.shape[2] // ntp
    rows = part * n
    groups = width // D
    gcols = FAN * D
    share = rows // nseq
    sec, seq, tp = lax.axis_index("section"), lax.axis_index("seq"), lax.axis_index("tp")
    me = seq * ntp + tp
    up, down = lax.rem(sec + 1, nsec), lax.rem(sec + nsec - 1, nsec)

    def dev(s, i):
        return {"section": s, "seq": lax.div(i, ntp), "tp": lax.rem(i, ntp)}

    def half(i):
        return pl.ds(pl.multiple_of(lax.rem(i, ntp) * width, width), width)

    loads = [
        pltpu.make_async_copy(c_hbm.at[0], c_vm, load_sem.at[0]),
        pltpu.make_async_copy(q_hbm.at[0], q_vm, load_sem.at[1]),
    ]
    for c in loads:
        c.start()
    mine = [
        pltpu.make_async_copy(k_hbm.at[0, :, half(me)], kg.at[me], own_sem.at[0]),
        pltpu.make_async_copy(v_hbm.at[0, :, half(me)], vg.at[me], own_sem.at[1]),
    ]
    for c in mine:
        c.start()

    barrier = pltpu.get_barrier_semaphore()
    for d in range(n):
        peer = lax.rem(me + d, n)
        pl.semaphore_signal(barrier, inc=1, device_id=dev(up, peer), device_id_type=MESH)
        pl.semaphore_signal(barrier, inc=1, device_id=dev(down, peer), device_id_type=MESH)
        if d > 0:
            pl.semaphore_signal(barrier, inc=1, device_id=dev(sec, peer), device_id_type=MESH)

    row_tile = lax.broadcasted_iota(jnp.int32, (rows, text), 0) // (rows // own.shape[1])
    blocks = pat.shape[1]
    lane_block = lax.broadcasted_iota(jnp.int32, (rows, text), 1) // (text // blocks)
    allowed = jnp.zeros((rows, text), jnp.bool_)
    for b in range(blocks):
        for t in range(own.shape[1]):
            owner = jnp.where(pat[0, b, t] > 0, own[0, t], -1)
            hit = row_tile == owner
            if blocks > 1:
                hit = hit & (lane_block == b)
            allowed = allowed | hit
    k_bd[...] = jnp.zeros_like(k_bd)
    v_bd[...] = jnp.zeros_like(v_bd)

    pl.semaphore_wait(barrier, 3 * n - 1)

    def remote(src, dst, ss, rs, to):
        return pltpu.make_async_remote_copy(
            src_ref=src, dst_ref=dst, send_sem=ss, recv_sem=rs, device_id=to, device_id_type=MESH
        )

    n_copies, k_copies, v_copies = [], [], []
    for d in range(n):
        peer = lax.rem(me + d, n)
        c = remote(v_hbm.at[0, :, half(peer)], ng.at[me], n_ss.at[d], n_rs.at[d], dev(up, peer))
        c.start()
        n_copies.append(c)
    for d in range(1, n):
        peer = lax.rem(me + d, n)
        c = remote(k_hbm.at[0, :, half(peer)], kg.at[me], k_ss.at[d], k_rs.at[d], dev(sec, peer))
        c.start()
        k_copies.append(c)
    for d in range(1, n):
        peer = lax.rem(me + d, n)
        c = remote(v_hbm.at[0, :, half(peer)], vg.at[me], v_ss.at[d], v_rs.at[d], dev(sec, peer))
        c.start()
        v_copies.append(c)

    def assemble(which, src):
        for i in range(n):
            asm[which, part * i : part * (i + 1), :] = src[i].astype(F32)

    def head(ref, g, h):
        j = g * FAN + h
        return ref[:, j * D : (j + 1) * D]

    for c in mine + loads:
        c.wait()
    for c in k_copies:
        c.wait_recv()
    assemble(0, kg)
    keys = [asm[0, :, g * D : (g + 1) * D].astype(BF16) for g in range(groups)]
    p_copies, dp_copies = [], []

    def probs_of(g):
        for h in range(FAN):
            s = nt(keys[g], head(q_vm, g, h)) * scale
            s = jnp.where(allowed, s, -jnp.inf)
            e = jnp.exp(s - jnp.max(s, axis=0, keepdims=True))
            p = e * (1.0 / jnp.sum(e, axis=0, keepdims=True))
            p_f32[g, h * rows : (h + 1) * rows, :] = p
            p_send[g, h * rows : (h + 1) * rows, :] = p.astype(BF16)
        c = remote(
            p_send.at[g], p_recv.at[g], p_ss.at[g], p_rs.at[g], dev(up, me)
        )
        c.start()
        p_copies.append(c)

    def dprobs_of(g, values):
        for h in range(FAN):
            dp = nt(values, head(c_vm, g, h))
            dp = dp - jnp.sum(dp, axis=0, keepdims=True) * (1.0 / rows)
            dp_send[g, h * rows : (h + 1) * rows, :] = dp.astype(BF16)
        c = remote(
            dp_send.at[g], dp_recv.at[g], dp_ss.at[g], dp_rs.at[g], dev(down, me)
        )
        c.start()
        dp_copies.append(c)

    probs_of(0)
    for c in n_copies:
        c.wait_recv()
    assemble(1, ng)
    for g in range(groups):
        dprobs_of(g, asm[1, :, g * D : (g + 1) * D].astype(BF16))
        if g + 1 < groups:
            probs_of(g + 1)

    for c in v_copies:
        c.wait_recv()
    assemble(2, vg)
    for g in range(groups):
        values = asm[2, :, g * D : (g + 1) * D].astype(BF16)
        for a in range(PACK):
            k_bd[g, a * rows : (a + 1) * rows, a * D : (a + 1) * D] = keys[g]
            v_bd[g, a * rows : (a + 1) * rows, a * D : (a + 1) * D] = values

    lot = PACK * rows
    wide = PACK * D
    for g in range(groups):
        for a in range(FAN // PACK):
            at = g * gcols + a * wide
            o = tn(p_send[g, a * lot : (a + 1) * lot, :], v_bd[g])
            att_vm[0, :, at : at + wide] = o.astype(BF16)

    dk_copies, dv_copies = [], []
    for g in range(groups):
        dp_copies[g].wait_recv()
        dk = jnp.zeros((rows, D), F32)
        ds_list = []
        for h in range(FAN):
            at = slice(h * rows, (h + 1) * rows)
            p = p_f32[g, at, :]
            dp = dp_recv[g, at, :].astype(F32)
            delta = jnp.sum(p * dp, axis=0, keepdims=True)
            ds = (p * (dp - delta)).astype(BF16)
            ds_list.append(ds)
            dk = dk + nn(ds, head(q_vm, g, h))
        dk_t[g] = dk * scale
        for d in range(1, nseq):
            to = lax.rem(seq + d, nseq)
            c = remote(
                dk_t.at[g, pl.ds(pl.multiple_of(to * share, share), share), :],
                dk_r.at[d, g], dk_ss.at[g, d], dk_rs.at[g, d],
                {"section": sec, "seq": to, "tp": tp},
            )
            c.start()
            dk_copies.append(c)
        p_copies[g].wait_recv()
        dv = jnp.zeros((rows, D), F32)
        for h in range(FAN):
            dv = dv + nn(p_recv[g, h * rows : (h + 1) * rows, :], head(c_vm, g, h))
        dv_t[g] = dv
        for d in range(nseq):
            to = lax.rem(seq + d, nseq)
            c = remote(
                dv_t.at[g, pl.ds(pl.multiple_of(to * share, share), share), :],
                dv_r.at[d, g], dv_ss.at[g, d], dv_rs.at[g, d],
                {"section": down, "seq": to, "tp": tp},
            )
            c.start()
            dv_copies.append(c)
        for a in range(FAN // PACK):
            at = g * gcols + a * wide
            ds = jnp.concatenate(ds_list[a * PACK : (a + 1) * PACK], axis=0)
            gq_vm[0, :, at : at + wide] = (tn(ds, k_bd[g]) * scale).astype(BF16)

    for c in dk_copies + dv_copies:
        c.wait_recv()
    for g in range(groups):
        dk = dk_t[g, pl.ds(pl.multiple_of(seq * share, share), share), :]
        for d in range(1, nseq):
            dk = dk + dk_r[d, g]
        dv = dv_r[0, g]
        for d in range(1, nseq):
            dv = dv + dv_r[d, g]
        gk_out[0, :, g * D : (g + 1) * D] = dk.astype(BF16)
        gv_out[0, :, g * D : (g + 1) * D] = dv.astype(BF16)
    for c in n_copies + k_copies + v_copies + p_copies + dp_copies + dk_copies + dv_copies:
        c.wait_send()


def put_out(*refs):
    sems = refs[8]
    copies = []
    for i in range(4):
        step = refs[i].shape[1] // CUTS if i < 2 else refs[i].shape[1]
        for j in range(refs[i].shape[1] // step):
            at = slice(j * step, (j + 1) * step)
            copies.append(
                pltpu.make_async_copy(refs[i].at[:, at], refs[4 + i].at[:, at], sems.at[i, j])
            )
    for c in copies:
        c.start()
    for c in copies:
        c.wait()


def per_device(nsec, nseq, ntp, queries, keys, values, cotangent, pattern, tile_owner):
    n = nseq * ntp
    part = keys.shape[1]
    width = keys.shape[2] // ntp
    rows = part * n
    groups = width // HEAD_SIZE
    text, cols = queries.shape[1:]
    share = rows // nseq
    D = HEAD_SIZE
    dma = pltpu.SemaphoreType.DMA
    vm = pltpu.VMEM
    anyspace = pl.BlockSpec(memory_space=pl.ANY)
    smem = pl.BlockSpec(memory_space=pltpu.SMEM)
    vmem = pl.BlockSpec(memory_space=pltpu.VMEM)
    results = pl.pallas_call(
        functools.partial(kernel, nsec, nseq, ntp),
        out_shape=(
            vm((1, text, cols), BF16),
            vm((1, text, cols), BF16),
            vm((1, share, width), BF16),
            vm((1, share, width), BF16),
        ),
        in_specs=[anyspace] * 4 + [smem] * 2,
        out_specs=(vmem,) * 4,
        scratch_shapes=[
            vm((text, cols), BF16),
            vm((text, cols), BF16),
            vm((n, part, width), BF16),
            vm((n, part, width), BF16),
            vm((n, part, width), BF16),
            vm((3, rows, width), F32),
            vm((groups, PACK * rows, PACK * D), BF16),
            vm((groups, PACK * rows, PACK * D), BF16),
            vm((groups, FAN * rows, text), F32),
            vm((groups, FAN * rows, text), BF16),
            vm((groups, FAN * rows, text), BF16),
            vm((groups, FAN * rows, text), BF16),
            vm((groups, FAN * rows, text), BF16),
            vm((groups, rows, D), F32),
            vm((groups, rows, D), F32),
            vm((nseq, groups, share, D), F32),
            vm((nseq, groups, share, D), F32),
            dma((2,)),
            dma((2,)),
            dma((n,)), dma((n,)), dma((n,)), dma((n,)), dma((n,)), dma((n,)),
            dma((groups,)), dma((groups,)), dma((groups,)), dma((groups,)),
            dma((groups, nseq)), dma((groups, nseq)), dma((groups, nseq)), dma((groups, nseq)),
        ],
        compiler_params=pltpu.CompilerParams(collective_id=0, has_side_effects=True),
        name="cross",
    )(queries, keys, values, cotangent, pattern, tile_owner)
    return pl.pallas_call(
        put_out,
        out_shape=tuple(jax.ShapeDtypeStruct(r.shape, r.dtype) for r in results),
        in_specs=[vmem] * 4,
        out_specs=(anyspace,) * 4,
        scratch_shapes=[dma((4, CUTS))],
        name="put",
    )(*[pltpu.with_memory_space_constraint(r, pltpu.VMEM) for r in results])


def solution(mesh):
    nsec, nseq, ntp = (mesh.shape[a] for a in ("section", "seq", "tp"))
    in_specs = (
        P("section", "seq", "tp"),
        P("section", ("seq", "tp"), None),
        P("section", ("seq", "tp"), None),
        P("section", "seq", "tp"),
        P("section", "seq", None),
        P("section", None),
    )
    out_specs = (P("section", "seq", "tp"),) * 4
    return jax.shard_map(
        functools.partial(per_device, nsec, nseq, ntp),
        mesh=mesh, in_specs=in_specs, out_specs=out_specs, check_vma=False,
    )
```
